512 devices in a mesh: dom: 128 (over y, z, core), field: 4 (over x).
Axes of the slice: x: 4, y: 4, z: 16, core: 2. Of those that a mesh axis runs over, the one named last changes fastest.
Arguments:
- adjoint: bfloat16 [1024, 384, 128], P('dom', 'field'), may hold values from -6 to 6
- face_blocks: bfloat16 [4480, 384, 384], P('dom', 'field'), may hold values from -0.3125 to 0.3125
- diag_blocks: bfloat16 [1024, 384, 384], P('dom', 'field'), may hold values from -0.3125 to 0.3125
- face_left: int32 [4480], P('dom'), may hold values from 0 to 7
- face_right: int32 [4480], P('dom'), may hold values from 0 to 7
- face_code: int32 [4480], P('dom'), may hold values from 0 to 7
- side_counts: int32 [128, 5], P('dom'), may hold values from 1 to 7, 24 in all within a row
Outputs:
- psi: bfloat16 [1024, 384, 128], P('dom', 'field')
- second: bfloat16 [1024, 384, 128], P('dom', 'field')
The draws below stay inside these ranges and needn't reach their ends.
Inputs may be any that keep to these rules, and one draw needn't show every extreme that they name: `side_counts`: the 5 lists of one partition hold 24 live faces together, each list at least one, and some list of every partition is full with 7. `face_right`: slots at or beyond a list's count are unused; their indices and blocks are arbitrary.
All inputs are finite; a program needn't handle non-finite values.
Results may differ from the reference program's by a relative error of at most 0.0049.
Values may be sent and summed in bfloat16 or wider, within the bound.
No kernel may reach another device: no remote copies, remote signals or barrier semaphores. Data moves between devices by JAX's collectives and lax.ppermute only.
A program may use at most 64 MiB of HBM per device.

```python
import math
import jax
import jax.numpy as jnp
import numpy as np
from jax import lax

PTS = 4
U = 384
E = 8
K = 128
NS = 5
CAP = 7
FACES = 24
SLOTS = 35
DOMAINS = 128
STRIDE = 16
ELEMS = 1024
FACE_SLOTS = 4480


def set_ends(drawn, rng, least, high):
    extent = drawn.shape
    spot = [jax.random.randint(jax.random.fold_in(rng, axis), (), 0, extent[axis]) for axis in range(len(extent))]
    drawn = drawn.at[tuple(spot)].set(least)
    longest = extent.index(max(extent))
    spot[longest] = (spot[longest] + 1) % extent[longest]
    return drawn.at[tuple(spot)].set(high)


def block_levels(own_key, dims, cuts, smallest, top_value):
    gain = 1.0
    for position, shards_of in cuts:
        heights = jax.random.uniform(jax.random.fold_in(jax.random.fold_in(own_key, 6), position), (shards_of,), jnp.float32, smallest / len(cuts), top_value / len(cuts))
        gain = gain * jnp.repeat(jnp.exp(heights), dims[position] // shards_of).reshape((-1,) + (1,) * (len(dims) - 1 - position))
    return gain


def profile(amount, total, most, lean):
    loads = [(1 << 20) // math.isqrt(rank ** lean) + 1 for rank in range(2, amount + 1)]
    rest, given = total - most - (amount - 1), [1] * (amount - 1)
    while rest > 0:
        free = [i for i in range(amount - 1) if given[i] < most]
        pool, remaining = sum([loads[i] for i in free]), rest
        for i in free:
            addition = min(most - given[i], max(1, remaining * loads[i] // pool), rest)
            given[i] = given[i] + addition
            rest = rest - addition
    return np.array([most] + given)


def uneven(own_key, count, total, limit, skew):
    if count == 2:
        one = jax.random.randint(own_key, (), max(1, total - limit), min(limit, total - 1) + 1)
        return jnp.stack([one, total - one])
    lengths = jnp.asarray(profile(count, total, limit, skew), jnp.int32)
    pairs = (count - 1) // 2
    source_of, sink = lengths[1:1 + 2 * pairs:2], lengths[2:2 + 2 * pairs:2]
    margin = jnp.minimum(source_of - 1, limit - sink)
    passed = jax.random.randint(jax.random.fold_in(own_key, 1), (pairs,), 0, 1 << 20) % (margin + 1)
    lengths = lengths.at[1:1 + 2 * pairs:2].set(source_of - passed).at[2:2 + 2 * pairs:2].set(sink + passed)
    return lengths[jax.random.permutation(jax.random.fold_in(own_key, 2), count)]


def scatter_about(rng, shape, width, reach, shards=(), held_as=jnp.bfloat16):
    result = width * jax.random.normal(rng, shape, jnp.float32)
    if shards:
        result = result * block_levels(rng, shape, shards, -0.22, 0.18)
    return jnp.clip(result, -reach, reach).astype(held_as)


def setup_inputs(seed: int = 0) -> dict:
    key_of = jax.random.split(jax.random.key(seed), 8)
    adjoint = scatter_about(key_of[0], (ELEMS, U, K), 1.0, 6.0, ((0, 128), (1, 4)))
    face_blocks = scatter_about(key_of[1], (FACE_SLOTS, U, U), U ** -0.5, 0.3125, ((0, 128), (1, 4)))
    diag_blocks = scatter_about(key_of[2], (ELEMS, U, U), U ** -0.5, 0.3125, ((0, 128), (1, 4)))
    face_left = set_ends(jax.random.randint(key_of[3], (FACE_SLOTS,), 0, E), jax.random.fold_in(key_of[3], 1), 0, E - 1).astype(jnp.int32)
    face_right = set_ends(jax.random.randint(key_of[4], (FACE_SLOTS,), 0, E), jax.random.fold_in(key_of[4], 1), 0, E - 1).astype(jnp.int32)
    face_code = set_ends(jax.random.randint(key_of[5], (FACE_SLOTS,), 0, 8), jax.random.fold_in(key_of[5], 1), 0, 7).astype(jnp.int32)
    side_counts = jax.vmap(lambda own: uneven(own, NS, FACES, CAP, 2))(jax.random.split(key_of[6], DOMAINS)).reshape((DOMAINS, NS)).astype(jnp.int32)
    return {"adjoint": adjoint, "face_blocks": face_blocks, "diag_blocks": diag_blocks, "face_left": face_left, "face_right": face_right, "face_code": face_code, "side_counts": side_counts}


def orient(product, orient_code):
    number = product.shape[0]
    shaped = product.reshape(number, product.shape[1] // (PTS * PTS), PTS, PTS, product.shape[2])
    flip_rows = ((orient_code % 2) == 1)[:, None, None, None, None]
    flip_cols = (((orient_code // 2) % 2) == 1)[:, None, None, None, None]
    swap_both = (orient_code >= 4)[:, None, None, None, None]
    shaped = jnp.where(flip_rows, jnp.flip(shaped, 2), shaped)
    shaped = jnp.where(flip_cols, jnp.flip(shaped, 3), shaped)
    shaped = jnp.where(swap_both, jnp.swapaxes(shaped, 2, 3), shaped)
    return shaped.reshape(product.shape)


def reference(adjoint, face_blocks, diag_blocks, face_left, face_right, face_code, side_counts):
    offsets = jnp.array([0, 1, -1, STRIDE, -STRIDE], dtype=jnp.int32)
    slot_side = (jnp.arange(SLOTS, dtype=jnp.int32) // CAP).astype(jnp.int32)
    slot_place = (jnp.arange(SLOTS, dtype=jnp.int32) % CAP).astype(jnp.int32)

    def apply_op(vector):
        def per_domain(domain, summed):
            domain = jnp.asarray(domain).astype(jnp.int32)
            start = (domain * SLOTS).astype(jnp.int32)
            blocks = lax.dynamic_slice_in_dim(face_blocks, start, SLOTS, 0).astype(jnp.float32)
            sources = lax.dynamic_slice_in_dim(face_left, start, SLOTS, 0)
            targets = lax.dynamic_slice_in_dim(face_right, start, SLOTS, 0)
            codes_here = lax.dynamic_slice_in_dim(face_code, start, SLOTS, 0)
            counts = lax.dynamic_slice_in_dim(side_counts, domain, 1, 0)[0]
            rows_full = jnp.take(vector, (domain * E + sources).astype(jnp.int32), axis=0).astype(jnp.float32)
            product = jnp.einsum('scr,srk->sck', blocks, rows_full)
            product = orient(product, codes_here)
            active = slot_place < counts[slot_side]
            product = jnp.where(active[:, None, None], product, jnp.float32(0.0))
            owner = jnp.mod(domain + offsets[slot_side], DOMAINS).astype(jnp.int32)
            summed = summed.at[(owner * E + targets).astype(jnp.int32)].add(product)
            estart = (domain * E).astype(jnp.int32)
            own_blocks = lax.dynamic_slice_in_dim(diag_blocks, estart, E, 0).astype(jnp.float32)
            own_rows = lax.dynamic_slice_in_dim(vector, estart, E, 0).astype(jnp.float32)
            own_term = jnp.einsum('ecr,erk->eck', own_blocks, own_rows)
            current = lax.dynamic_slice_in_dim(summed, estart, E, 0)
            return lax.dynamic_update_slice_in_dim(summed, current + own_term, estart, 0)

        initial = jnp.zeros((ELEMS, U, K), dtype=jnp.float32)
        return lax.fori_loop(0, DOMAINS, per_domain, initial)

    first = apply_op(adjoint)
    psi = (adjoint.astype(jnp.float32) - 0.5 * first).astype(jnp.bfloat16)
    second = apply_op(psi).astype(jnp.bfloat16)
    return psi, second
```

```python
import jax
import jax.numpy as jnp
from jax import lax
from jax.experimental import pallas as pl
from jax.experimental.pallas import tpu as pltpu
from jax.sharding import PartitionSpec as P

PTS = 4
NS = 5
CELL = PTS * PTS


def from_behind(array, axis, by):
    peers = lax.axis_size(axis)
    return lax.ppermute(array, axis, [(i, (i + by) % peers) for i in range(peers)])


def source_rows(code, shape):
    row = lax.broadcasted_iota(jnp.int32, shape, 0)
    j, k = row // PTS, row % PTS
    swap = code >= 4
    a = jnp.where(swap, k, j)
    b = jnp.where(swap, j, k)
    j2 = jnp.where(code % 2 == 1, PTS - 1 - a, a)
    k2 = jnp.where((code // 2) % 2 == 1, PTS - 1 - b, b)
    return j2 * PTS + k2


def oriented(product, code):
    lanes = product.shape[1]
    source = source_rows(code, (CELL, lanes))
    out = []
    for group in range(product.shape[0] // CELL):
        low = product[group * CELL : group * CELL + 8]
        high = product[group * CELL + 8 : (group + 1) * CELL]
        for half in range(2):
            want = source[half * 8 : half * 8 + 8]
            spot = want % 8
            out.append(
                jnp.where(
                    want < 8,
                    jnp.take_along_axis(low, spot, axis=0),
                    jnp.take_along_axis(high, spot, axis=0),
                )
            )
    return jnp.concatenate(out, 0)


def side_into(acc, side, capacity, block_ref, x_ref, left, right, code, counts):
    n_elems = x_ref.shape[0]
    for c in range(capacity):
        slot = side * capacity + c
        product = jnp.dot(block_ref[c], x_ref[left[slot] & 7], preferred_element_type=jnp.float32)
        product = oriented(product, code[slot] & 7)
        target = jnp.where(c < counts[0, side], right[slot] & 7, n_elems)
        acc[target] += product


def far_kernel(left, right, code, counts, x_ref, up_ref, down_ref, up_out, down_out, acc):
    capacity, n_elems = up_ref.shape[0], x_ref.shape[0]
    for side, block_ref, out in ((3, up_ref, up_out), (4, down_ref, down_out)):
        acc[...] = jnp.zeros_like(acc)
        side_into(acc, side, capacity, block_ref, x_ref, left, right, code, counts)
        out[...] = acc[:n_elems].astype(out.dtype)


def near_kernel(left, right, code, counts, x_ref, diag_ref, own_ref, up_ref, down_ref, own_out, up_out, down_out, acc):
    capacity, n_elems = own_ref.shape[0], x_ref.shape[0]
    for side, block_ref, out in ((1, up_ref, up_out), (2, down_ref, down_out)):
        acc[...] = jnp.zeros_like(acc)
        side_into(acc, side, capacity, block_ref, x_ref, left, right, code, counts)
        out[...] = acc[:n_elems].astype(out.dtype)
    for e in range(n_elems):
        acc[e] = jnp.dot(diag_ref[e], x_ref[e], preferred_element_type=jnp.float32)
    side_into(acc, 0, capacity, own_ref, x_ref, left, right, code, counts)
    own_out[...] = acc[:n_elems]


def local(adjoint, face_blocks, diag_blocks, face_left, face_right, face_code, side_counts):
    n_domains = lax.axis_size("dom")
    stride = n_domains // 8
    capacity = face_blocks.shape[0] // NS
    n_elems, rows, lanes = adjoint.shape
    width = face_blocks.shape[2]
    scalars = [pl.BlockSpec(memory_space=pltpu.SMEM)] * 4
    whole_spec = pl.BlockSpec((n_elems, width, lanes), lambda i: (0, 0, 0))
    diag_spec = pl.BlockSpec((n_elems, rows, width), lambda i: (0, 0, 0))
    out_spec = pl.BlockSpec((n_elems, rows, lanes), lambda i: (0, 0, 0))
    sums = jax.ShapeDtypeStruct((n_elems, rows, lanes), jnp.bfloat16)
    totals = jax.ShapeDtypeStruct((n_elems, rows, lanes), jnp.float32)
    acc = pltpu.VMEM((n_elems + 1, rows, lanes), jnp.float32)

    def side_spec(side):
        return pl.BlockSpec((capacity, rows, width), lambda i: (side, 0, 0))

    def cost(blocks):
        return pl.CostEstimate(
            flops=2 * blocks * rows * width * lanes,
            bytes_accessed=2 * blocks * rows * width,
            transcendentals=0,
        )

    far = pl.pallas_call(
        far_kernel,
        grid=(1,),
        in_specs=scalars + [whole_spec, side_spec(3), side_spec(4)],
        out_specs=[out_spec] * 2,
        out_shape=[sums] * 2,
        scratch_shapes=[acc],
        cost_estimate=cost(2 * capacity),
        name="far_sides",
    )
    near = pl.pallas_call(
        near_kernel,
        grid=(1,),
        in_specs=scalars + [whole_spec, diag_spec, side_spec(0), side_spec(1), side_spec(2)],
        out_specs=[out_spec] * 3,
        out_shape=[totals, sums, sums],
        scratch_shapes=[acc],
        cost_estimate=cost(3 * capacity + n_elems),
        name="near_sides",
    )
    tables = (face_left, face_right, face_code, side_counts)

    def apply_op(vector):
        whole = lax.all_gather(vector, "field", axis=1, tiled=True)
        far_up, far_down = far(*tables, whole, face_blocks, face_blocks)
        far_up = from_behind(far_up, "dom", stride)
        far_down = from_behind(far_down, "dom", -stride)
        own, up, down = near(*tables, whole, diag_blocks, face_blocks, face_blocks, face_blocks)
        up = from_behind(up, "dom", 1)
        down = from_behind(down, "dom", -1)
        return own + up + down + far_up + far_down

    first = apply_op(adjoint)
    psi = (adjoint.astype(jnp.float32) - 0.5 * first).astype(jnp.bfloat16)
    second = apply_op(psi).astype(jnp.bfloat16)
    return (psi, second)


def solution(mesh):
    return jax.shard_map(
        local,
        mesh=mesh,
        in_specs=(
            P("dom", "field", None),
            P("dom", "field", None),
            P("dom", "field", None),
            P("dom"),
            P("dom"),
            P("dom"),
            P("dom", None),
        ),
        out_specs=(P("dom", "field", None), P("dom", "field", None)),
        check_vma=False,
    )
```

```python
from functools import partial

import jax
import jax.numpy as jnp
from jax import lax
from jax.experimental import pallas as pl
from jax.experimental.pallas import tpu as pltpu
from jax.sharding import PartitionSpec as P

PTS = 4
NS = 5
CELL = PTS * PTS


def from_behind(array, axis, by):
    peers = lax.axis_size(axis)
    return lax.ppermute(array, axis, [(i, (i + by) % peers) for i in range(peers)])


def source_rows(code, shape):
    row = lax.broadcasted_iota(jnp.int32, shape, 0)
    j, k = row // PTS, row % PTS
    swap = code >= 4
    a = jnp.where(swap, k, j)
    b = jnp.where(swap, j, k)
    j2 = jnp.where(code % 2 == 1, PTS - 1 - a, a)
    k2 = jnp.where((code // 2) % 2 == 1, PTS - 1 - b, b)
    return j2 * PTS + k2


def oriented(product, code):
    lanes = product.shape[1]
    source = source_rows(code, (CELL, lanes))
    out = []
    for group in range(product.shape[0] // CELL):
        low = product[group * CELL : group * CELL + 8]
        high = product[group * CELL + 8 : (group + 1) * CELL]
        for half in range(2):
            want = source[half * 8 : half * 8 + 8]
            spot = want % 8
            out.append(
                jnp.where(
                    want < 8,
                    jnp.take_along_axis(low, spot, axis=0),
                    jnp.take_along_axis(high, spot, axis=0),
                )
            )
    return jnp.concatenate(out, 0)


def side_sum(acc, place, block_ref, x_ref, tables):
    left, right, code, counts, sides = tables
    capacity, n_elems = block_ref.shape[0], x_ref.shape[0]
    side = sides[place]
    for c in range(capacity):
        slot = side * capacity + c
        product = jnp.dot(block_ref[c], x_ref[left[slot] & 7], preferred_element_type=jnp.float32)
        product = oriented(product, code[slot] & 7)
        target = jnp.where(c < counts[0, side], right[slot] & 7, n_elems)
        acc[target] += product


def side_kernel(place, *refs):
    tables, (x_ref, block_ref, out, acc) = refs[:5], refs[5:]
    acc[...] = jnp.zeros_like(acc)
    side_sum(acc, place, block_ref, x_ref, tables)
    out[...] = acc[: x_ref.shape[0]].astype(out.dtype)


def near_kernel(*refs):
    tables, (x_ref, up_ref, down_ref, up_out, down_out, acc) = refs[:5], refs[5:]
    for place, block_ref, out in ((1, up_ref, up_out), (2, down_ref, down_out)):
        acc[...] = jnp.zeros_like(acc)
        side_sum(acc, place, block_ref, x_ref, tables)
        out[...] = acc[: x_ref.shape[0]].astype(out.dtype)


def own_kernel(*refs):
    tables, (x_ref, diag_ref, block_ref, out, acc) = refs[:5], refs[5:]
    n_elems = x_ref.shape[0]
    for e in range(n_elems):
        acc[e] = jnp.dot(diag_ref[e], x_ref[e], preferred_element_type=jnp.float32)
    side_sum(acc, 0, block_ref, x_ref, tables)
    out[...] = acc[:n_elems]


def local(adjoint, face_blocks, diag_blocks, face_left, face_right, face_code, side_counts):
    n_domains = lax.axis_size("dom")
    stride = n_domains // 8
    capacity = face_blocks.shape[0] // NS
    n_elems, rows, lanes = adjoint.shape
    width = face_blocks.shape[2]
    half = lax.rem(lax.axis_index("dom") // stride, 2)
    sides = jnp.stack([0, 1, 2, 3 + half, 4 - half]).astype(jnp.int32)
    tables = (face_left, face_right, face_code, side_counts, sides)

    whole_spec = pl.BlockSpec((n_elems, width, lanes), lambda i, *t: (0, 0, 0))
    diag_spec = pl.BlockSpec((n_elems, rows, width), lambda i, *t: (0, 0, 0))
    out_spec = pl.BlockSpec((n_elems, rows, lanes), lambda i, *t: (0, 0, 0))
    sums = jax.ShapeDtypeStruct((n_elems, rows, lanes), jnp.bfloat16)
    totals = jax.ShapeDtypeStruct((n_elems, rows, lanes), jnp.float32)

    def side_spec(place):
        return pl.BlockSpec((capacity, rows, width), lambda i, *t: (t[4][place], 0, 0))

    def call(kernel, in_specs, out_shape, blocks):
        return pl.pallas_call(
            kernel,
            grid_spec=pltpu.PrefetchScalarGridSpec(
                num_scalar_prefetch=5,
                grid=(1,),
                in_specs=in_specs,
                out_specs=[out_spec] * len(out_shape),
                scratch_shapes=[pltpu.VMEM((n_elems + 1, rows, lanes), jnp.float32)],
            ),
            out_shape=out_shape,
            cost_estimate=pl.CostEstimate(
                flops=2 * blocks * rows * width * lanes,
                bytes_accessed=2 * blocks * rows * width,
                transcendentals=0,
            ),
        )

    keep = call(partial(side_kernel, 3), [whole_spec, side_spec(3)], [totals], capacity)
    pass_on = call(partial(side_kernel, 4), [whole_spec, side_spec(4)], [sums], capacity)
    near = call(near_kernel, [whole_spec, side_spec(1), side_spec(2)], [sums] * 2, 2 * capacity)
    own = call(own_kernel, [whole_spec, diag_spec, side_spec(0)], [totals], n_elems + capacity)
    ring = [(i, (i + (4 * (i // stride % 2) - 2) * stride) % n_domains) for i in range(n_domains)]
    across = [(i, (i + stride) % (2 * stride) + i // (2 * stride) * 2 * stride) for i in range(n_domains)]

    def apply_op(vector):
        whole = lax.all_gather(vector, "field", axis=1, tiled=True)
        (passed,) = pass_on(*tables, whole, face_blocks)
        passed = lax.ppermute(passed, "dom", ring)
        (kept,) = keep(*tables, whole, face_blocks)
        joined = (kept + passed).astype(jnp.bfloat16)
        far = lax.ppermute(joined, "dom", across)
        up, down = near(*tables, whole, face_blocks, face_blocks)
        up = from_behind(up, "dom", 1)
        down = from_behind(down, "dom", -1)
        (total,) = own(*tables, whole, diag_blocks, face_blocks)
        return total, up, down, far

    total, up, down, far = apply_op(adjoint)
    base = adjoint.astype(jnp.float32) - 0.5 * (total + up + down)
    psi = (base - 0.5 * far).astype(jnp.bfloat16)
    total, up, down, far = apply_op(psi)
    base = total + up + down
    second = (base + far).astype(jnp.bfloat16)
    return (psi, second)


def solution(mesh):
    return jax.shard_map(
        local,
        mesh=mesh,
        in_specs=(
            P("dom", "field", None),
            P("dom", "field", None),
            P("dom", "field", None),
            P("dom"),
            P("dom"),
            P("dom"),
            P("dom", None),
        ),
        out_specs=(P("dom", "field", None), P("dom", "field", None)),
        check_vma=False,
    )
```

```python
import jax
import jax.numpy as jnp
from jax import lax
from jax.experimental import pallas as pl
from jax.experimental.pallas import tpu as pltpu
from jax.sharding import PartitionSpec as P

PTS = 4
NS = 5
CELL = PTS * PTS


def upper_half():
    stride = lax.axis_size("dom") // 8
    return lax.rem(lax.div(lax.axis_index("dom"), stride), 2)


def source_rows(code, shape):
    row = lax.broadcasted_iota(jnp.int32, shape, 0)
    j, k = row // PTS, row % PTS
    swap = code >= 4
    a = jnp.where(swap, k, j)
    b = jnp.where(swap, j, k)
    j2 = jnp.where(code % 2 == 1, PTS - 1 - a, a)
    k2 = jnp.where((code // 2) % 2 == 1, PTS - 1 - b, b)
    return j2 * PTS + k2


def oriented(product, code):
    lanes = product.shape[1]
    source = source_rows(code, (CELL, lanes))
    out = []
    for group in range(product.shape[0] // CELL):
        low = product[group * CELL : group * CELL + 8]
        high = product[group * CELL + 8 : (group + 1) * CELL]
        for half in range(2):
            want = source[half * 8 : half * 8 + 8]
            spot = want % 8
            out.append(
                jnp.where(
                    want < 8,
                    jnp.take_along_axis(low, spot, axis=0),
                    jnp.take_along_axis(high, spot, axis=0),
                )
            )
    return jnp.concatenate(out, 0)


def side_sum(acc, side, first, capacity, tables, block_ref, x_ref):
    left, right, code, counts = tables
    n_elems = x_ref.shape[0]
    for c in range(capacity):
        slot = side * capacity + c
        product = jnp.dot(block_ref[first + c], x_ref[left[slot] & 7], preferred_element_type=jnp.float32)
        target = jnp.where(c < counts[0, side], right[slot] & 7, n_elems)
        acc[target] += oriented(product, code[slot] & 7)


def out_sides():
    half, core = upper_half(), lax.rem(lax.axis_index("dom"), 2)
    return 4 - half, 2 - core, 1 + core, 3 + half


def send_kernel(*refs):
    tables, (x_ref, block_ref), outs, acc = refs[:4], refs[4:6], refs[6:10], refs[10]
    n_elems, capacity = x_ref.shape[0], block_ref.shape[0] // NS
    for side, out in zip(out_sides(), outs):
        acc[...] = jnp.zeros_like(acc)
        side_sum(acc, side, side * capacity, capacity, tables, block_ref, x_ref)
        out[...] = acc[:n_elems].astype(out.dtype)


def fetch_send_kernel(*refs):
    sources, (x_ref, block_ref), outs, (acc, held, *tables), sem = refs[:4], refs[4:6], refs[6:10], refs[10:16], refs[16]
    n_elems, capacity = x_ref.shape[0], block_ref.shape[0] // NS
    sides = out_sides()
    copies = [pltpu.make_async_copy(a, b, sem.at[i]) for i, (a, b) in enumerate(zip(sources, tables))]
    for place, side in enumerate(sides):
        lists = pl.ds(side * capacity, capacity)
        copies.append(pltpu.make_async_copy(block_ref.at[lists], held.at[pl.ds(place * capacity, capacity)], sem.at[4 + place]))
    for copy in copies:
        copy.start()
    for copy in copies[:4]:
        copy.wait()
    for place, (side, out) in enumerate(zip(sides, outs)):
        acc[...] = jnp.zeros_like(acc)
        copies[4 + place].wait()
        side_sum(acc, side, place * capacity, capacity, tables, held, x_ref)
        out[...] = acc[:n_elems].astype(out.dtype)


def own_kernel(*refs):
    tables, (x_ref, diag_ref, block_ref, out, acc) = refs[:4], refs[4:]
    n_elems = x_ref.shape[0]
    for e in range(n_elems):
        acc[e] = jnp.dot(diag_ref[e], x_ref[e], preferred_element_type=jnp.float32)
    side_sum(acc, 0, 0, block_ref.shape[0] // NS, tables, block_ref, x_ref)
    out[...] = acc[:n_elems]


def local(adjoint, face_blocks, diag_blocks, face_left, face_right, face_code, side_counts):
    n_domains = lax.axis_size("dom")
    stride = n_domains // 8
    capacity = face_blocks.shape[0] // NS
    n_elems, rows, lanes = adjoint.shape
    width = face_blocks.shape[2]
    tables = (face_left, face_right, face_code, side_counts)
    sums = jax.ShapeDtypeStruct((n_elems, rows, lanes), jnp.bfloat16)
    totals = jax.ShapeDtypeStruct((n_elems, rows, lanes), jnp.float32)

    def call(kernel, in_specs, out_shape, blocks, scratch=()):
        return pl.pallas_call(
            kernel,
            in_specs=in_specs,
            out_specs=[vmem] * len(out_shape),
            scratch_shapes=[pltpu.VMEM((n_elems + 1, rows, lanes), jnp.float32), *scratch],
            out_shape=out_shape,
            cost_estimate=pl.CostEstimate(
                flops=2 * blocks * rows * width * lanes,
                bytes_accessed=2 * blocks * rows * width,
                transcendentals=0,
            ),
            compiler_params=pltpu.CompilerParams(vmem_limit_bytes=8 << 20),
        )

    vmem, away = pl.BlockSpec(memory_space=pltpu.VMEM), pl.BlockSpec(memory_space=pltpu.HBM)
    lists = [pl.BlockSpec(memory_space=pltpu.SMEM)] * 4
    fetched = [
        pltpu.VMEM((4 * capacity, rows, width), jnp.bfloat16),
        *(pltpu.SMEM(a.shape, a.dtype) for a in tables),
        pltpu.SemaphoreType.DMA((8,)),
    ]
    outs = [sums] * 3 + [totals]
    fetch_send = call(fetch_send_kernel, [away] * 4 + [vmem, away], outs, 4 * capacity, fetched)
    send = call(send_kernel, lists + [vmem] * 2, outs, 4 * capacity)
    own = call(own_kernel, lists + [vmem] * 3, [totals], n_elems + capacity)
    ring = [(i, (i + (4 * (i // stride % 2) - 2) * stride) % n_domains) for i in range(n_domains)]
    across = [(i, (i + stride) % (2 * stride) + i // (2 * stride) * 2 * stride) for i in range(n_domains)]
    off_chip = [(i, (i + 2 * (i % 2) - 1) % n_domains) for i in range(n_domains)]
    on_chip = [(i, i + 1 - 2 * (i % 2)) for i in range(n_domains)]
    blocks = pltpu.with_memory_space_constraint(face_blocks, pltpu.VMEM)
    far_off = [pltpu.with_memory_space_constraint(a, pltpu.HBM) for a in (*tables, face_blocks)]
    diag = pltpu.with_memory_space_constraint(diag_blocks, pltpu.VMEM)

    def apply_op(vector, fetch):
        whole = lax.all_gather(vector, "field", axis=1, tiled=True)
        whole = pltpu.with_memory_space_constraint(whole, pltpu.VMEM)
        sent = fetch_send(*far_off[:4], whole, far_off[4]) if fetch else send(*tables, whole, blocks)
        passed, off, on, kept = sent
        passed = lax.ppermute(passed, "dom", ring)
        off = lax.ppermute(off, "dom", off_chip)
        on = lax.ppermute(on, "dom", on_chip)
        joined = (kept + passed).astype(jnp.bfloat16)
        far = lax.ppermute(joined, "dom", across)
        (total,) = own(*tables, whole, diag, blocks)
        return total + off + on + far

    first = apply_op(adjoint, True)
    psi = (adjoint.astype(jnp.float32) - 0.5 * first).astype(jnp.bfloat16)
    second = apply_op(psi, False).astype(jnp.bfloat16)
    return (psi, second)


def solution(mesh):
    return jax.shard_map(
        local,
        mesh=mesh,
        in_specs=(
            P("dom", "field", None),
            P("dom", "field", None),
            P("dom", "field", None),
            P("dom"),
            P("dom"),
            P("dom"),
            P("dom", None),
        ),
        out_specs=(P("dom", "field", None), P("dom", "field", None)),
        check_vma=False,
    )
```

```python
import jax
import jax.numpy as jnp
from jax import lax
from jax.experimental import pallas as pl
from jax.experimental.pallas import tpu as pltpu
from jax.sharding import PartitionSpec as P

PTS = 4
NS = 5
CELL = PTS * PTS


def upper_half():
    stride = lax.axis_size("dom") // 8
    return lax.rem(lax.div(lax.axis_index("dom"), stride), 2)


def source_rows(code, shape):
    row = lax.broadcasted_iota(jnp.int32, shape, 0)
    j, k = row // PTS, row % PTS
    swap = code >= 4
    a = jnp.where(swap, k, j)
    b = jnp.where(swap, j, k)
    j2 = jnp.where(code % 2 == 1, PTS - 1 - a, a)
    k2 = jnp.where((code // 2) % 2 == 1, PTS - 1 - b, b)
    return j2 * PTS + k2


def oriented(product, code):
    lanes = product.shape[1]
    source = source_rows(code, (CELL, lanes))
    out = []
    for group in range(product.shape[0] // CELL):
        low = product[group * CELL : group * CELL + 8]
        high = product[group * CELL + 8 : (group + 1) * CELL]
        for half in range(2):
            want = source[half * 8 : half * 8 + 8]
            spot = want % 8
            out.append(
                jnp.where(
                    want < 8,
                    jnp.take_along_axis(low, spot, axis=0),
                    jnp.take_along_axis(high, spot, axis=0),
                )
            )
    return jnp.concatenate(out, 0)


def side_sum(acc, side, first, capacity, tables, block_ref, x_ref):
    left, right, code, counts = tables
    n_elems = x_ref.shape[0]
    for c in range(capacity):
        slot = side * capacity + c
        product = jnp.dot(block_ref[first + c], x_ref[left[slot] & 7], preferred_element_type=jnp.float32)
        target = jnp.where(c < counts[0, side], right[slot] & 7, n_elems)
        acc[target] += oriented(product, code[slot] & 7)


def pass_kernel(*refs):
    tables, (x_ref, block_ref, out, acc) = refs[:4], refs[4:]
    n_elems, capacity = x_ref.shape[0], block_ref.shape[0] // NS
    side = 4 - upper_half()
    acc[...] = jnp.zeros_like(acc)
    side_sum(acc, side, side * capacity, capacity, tables, block_ref, x_ref)
    out[...] = acc[:n_elems].astype(out.dtype)


def fetch_pass_kernel(*refs):
    sources, (x_ref, block_ref, out, acc, held), tables, sem = refs[:4], refs[4:9], refs[9:13], refs[13]
    n_elems, capacity = x_ref.shape[0], block_ref.shape[0] // NS
    side = 4 - upper_half()
    copies = [pltpu.make_async_copy(a, b, sem.at[i]) for i, (a, b) in enumerate(zip(sources, tables))]
    copies.append(pltpu.make_async_copy(block_ref.at[pl.ds(side * capacity, capacity)], held, sem.at[4]))
    for copy in copies:
        copy.start()
    acc[...] = jnp.zeros_like(acc)
    for copy in copies:
        copy.wait()
    side_sum(acc, side, 0, capacity, tables, held, x_ref)
    out[...] = acc[:n_elems].astype(out.dtype)


def rest_kernel(*refs):
    tables, (x_ref, block_ref), outs, acc = refs[:4], refs[4:6], refs[6:9], refs[9]
    n_elems, capacity = x_ref.shape[0], block_ref.shape[0] // NS
    for side, out in zip((1, 2, 3 + upper_half()), outs):
        acc[...] = jnp.zeros_like(acc)
        side_sum(acc, side, side * capacity, capacity, tables, block_ref, x_ref)
        out[...] = acc[:n_elems].astype(out.dtype)


def own_kernel(*refs):
    tables, (x_ref, diag_ref, block_ref, out, acc) = refs[:4], refs[4:]
    n_elems = x_ref.shape[0]
    for e in range(n_elems):
        acc[e] = jnp.dot(diag_ref[e], x_ref[e], preferred_element_type=jnp.float32)
    side_sum(acc, 0, 0, block_ref.shape[0] // NS, tables, block_ref, x_ref)
    out[...] = acc[:n_elems]


def local(adjoint, face_blocks, diag_blocks, face_left, face_right, face_code, side_counts):
    n_domains = lax.axis_size("dom")
    stride = n_domains // 8
    capacity = face_blocks.shape[0] // NS
    n_elems, rows, lanes = adjoint.shape
    width = face_blocks.shape[2]
    tables = (face_left, face_right, face_code, side_counts)
    sums = jax.ShapeDtypeStruct((n_elems, rows, lanes), jnp.bfloat16)
    totals = jax.ShapeDtypeStruct((n_elems, rows, lanes), jnp.float32)

    def call(kernel, in_specs, out_shape, blocks, scratch=()):
        return pl.pallas_call(
            kernel,
            in_specs=in_specs,
            out_specs=[vmem] * len(out_shape),
            scratch_shapes=[pltpu.VMEM((n_elems + 1, rows, lanes), jnp.float32), *scratch],
            out_shape=out_shape,
            cost_estimate=pl.CostEstimate(
                flops=2 * blocks * rows * width * lanes,
                bytes_accessed=2 * blocks * rows * width,
                transcendentals=0,
            ),
            compiler_params=pltpu.CompilerParams(vmem_limit_bytes=8 << 20),
        )

    vmem, away = pl.BlockSpec(memory_space=pltpu.VMEM), pl.BlockSpec(memory_space=pltpu.HBM)
    lists = [pl.BlockSpec(memory_space=pltpu.SMEM)] * 4
    fetched = [
        pltpu.VMEM((capacity, rows, width), jnp.bfloat16),
        *(pltpu.SMEM(a.shape, a.dtype) for a in tables),
        pltpu.SemaphoreType.DMA((5,)),
    ]
    fetch_pass = call(fetch_pass_kernel, [away] * 4 + [vmem, away], [sums], capacity, fetched)
    pass_on = call(pass_kernel, lists + [vmem] * 2, [sums], capacity)
    rest = call(rest_kernel, lists + [vmem] * 2, [sums] * 2 + [totals], 3 * capacity)
    own = call(own_kernel, lists + [vmem] * 3, [totals], n_elems + capacity)
    ring = [(i, (i + (4 * (i // stride % 2) - 2) * stride) % n_domains) for i in range(n_domains)]
    across = [(i, (i + stride) % (2 * stride) + i // (2 * stride) * 2 * stride) for i in range(n_domains)]
    after = [(i, (i + 1) % n_domains) for i in range(n_domains)]
    before = [(i, (i - 1) % n_domains) for i in range(n_domains)]
    blocks = pltpu.with_memory_space_constraint(face_blocks, pltpu.VMEM)
    far_off = [pltpu.with_memory_space_constraint(a, pltpu.HBM) for a in (*tables, face_blocks)]
    diag = pltpu.with_memory_space_constraint(diag_blocks, pltpu.VMEM)

    def apply_op(vector, fetch):
        whole = lax.all_gather(vector, "field", axis=1, tiled=True)
        whole = pltpu.with_memory_space_constraint(whole, pltpu.VMEM)
        (passed,) = fetch_pass(*far_off[:4], whole, far_off[4]) if fetch else pass_on(*tables, whole, blocks)
        passed = lax.ppermute(passed, "dom", ring)
        up, down, kept = rest(*tables, whole, blocks)
        up = lax.ppermute(up, "dom", after)
        down = lax.ppermute(down, "dom", before)
        joined = (kept + passed).astype(jnp.bfloat16)
        far = lax.ppermute(joined, "dom", across)
        (total,) = own(*tables, whole, diag, blocks)
        return total + up + down + far

    first = apply_op(adjoint, True)
    psi = (adjoint.astype(jnp.float32) - 0.5 * first).astype(jnp.bfloat16)
    second = apply_op(psi, False).astype(jnp.bfloat16)
    return (psi, second)


def solution(mesh):
    return jax.shard_map(
        local,
        mesh=mesh,
        in_specs=(
            P("dom", "field", None),
            P("dom", "field", None),
            P("dom", "field", None),
            P("dom"),
            P("dom"),
            P("dom"),
            P("dom", None),
        ),
        out_specs=(P("dom", "field", None), P("dom", "field", None)),
        check_vma=False,
    )
```

```python
import jax
import jax.numpy as jnp
from jax import lax
from jax.experimental import pallas as pl
from jax.experimental.pallas import tpu as pltpu
from jax.sharding import PartitionSpec as P

PTS = 4
NS = 5
CELL = PTS * PTS


def upper_half():
    stride = lax.axis_size("dom") // 8
    return lax.rem(lax.div(lax.axis_index("dom"), stride), 2)


def source_rows(code, shape):
    row = lax.broadcasted_iota(jnp.int32, shape, 0)
    j, k = row // PTS, row % PTS
    swap = code >= 4
    a = jnp.where(swap, k, j)
    b = jnp.where(swap, j, k)
    j2 = jnp.where(code % 2 == 1, PTS - 1 - a, a)
    k2 = jnp.where((code // 2) % 2 == 1, PTS - 1 - b, b)
    return j2 * PTS + k2


def oriented(product, code):
    lanes = product.shape[1]
    source = source_rows(code, (CELL, lanes))
    out = []
    for group in range(product.shape[0] // CELL):
        low = product[group * CELL : group * CELL + 8]
        high = product[group * CELL + 8 : (group + 1) * CELL]
        for half in range(2):
            want = source[half * 8 : half * 8 + 8]
            spot = want % 8
            out.append(
                jnp.where(
                    want < 8,
                    jnp.take_along_axis(low, spot, axis=0),
                    jnp.take_along_axis(high, spot, axis=0),
                )
            )
    return jnp.concatenate(out, 0)


def side_sum(acc, side, first, capacity, tables, block_ref, x_ref):
    left, right, code, counts = tables
    n_elems = x_ref.shape[0]
    for c in range(capacity):
        slot = side * capacity + c
        product = jnp.dot(block_ref[first + c], x_ref[left[slot] & 7], preferred_element_type=jnp.float32)
        target = jnp.where(c < counts[0, side], right[slot] & 7, n_elems)
        acc[target] += oriented(product, code[slot] & 7)


def pass_kernel(*refs):
    tables, (x_ref, block_ref, out, acc) = refs[:4], refs[4:]
    n_elems, capacity = x_ref.shape[0], block_ref.shape[0] // NS
    side = 4 - upper_half()
    acc[...] = jnp.zeros_like(acc)
    side_sum(acc, side, side * capacity, capacity, tables, block_ref, x_ref)
    out[...] = acc[:n_elems].astype(out.dtype)


def fetch_pass_kernel(*refs):
    sources, (x_ref, block_ref, out, acc, held), tables, sem = refs[:4], refs[4:9], refs[9:13], refs[13]
    n_elems, capacity = x_ref.shape[0], block_ref.shape[0] // NS
    side = 4 - upper_half()
    copies = [pltpu.make_async_copy(a, b, sem.at[i]) for i, (a, b) in enumerate(zip(sources, tables))]
    copies.append(pltpu.make_async_copy(block_ref.at[pl.ds(side * capacity, capacity)], held, sem.at[4]))
    for copy in copies:
        copy.start()
    acc[...] = jnp.zeros_like(acc)
    for copy in copies:
        copy.wait()
    side_sum(acc, side, 0, capacity, tables, held, x_ref)
    out[...] = acc[:n_elems].astype(out.dtype)


def rest_sides():
    core = lax.rem(lax.axis_index("dom"), 2)
    return 2 - core, 1 + core, 3 + upper_half()


def rest_kernel(*refs):
    tables, (x_ref, block_ref), outs, acc = refs[:4], refs[4:6], refs[6:9], refs[9]
    n_elems, capacity = x_ref.shape[0], block_ref.shape[0] // NS
    for side, out in zip(rest_sides(), outs):
        acc[...] = jnp.zeros_like(acc)
        side_sum(acc, side, side * capacity, capacity, tables, block_ref, x_ref)
        out[...] = acc[:n_elems].astype(out.dtype)


def own_kernel(*refs):
    tables, (x_ref, diag_ref, block_ref, out, acc) = refs[:4], refs[4:]
    n_elems = x_ref.shape[0]
    for e in range(n_elems):
        acc[e] = jnp.dot(diag_ref[e], x_ref[e], preferred_element_type=jnp.float32)
    side_sum(acc, 0, 0, block_ref.shape[0] // NS, tables, block_ref, x_ref)
    out[...] = acc[:n_elems]


def local(adjoint, face_blocks, diag_blocks, face_left, face_right, face_code, side_counts):
    n_domains = lax.axis_size("dom")
    stride = n_domains // 8
    capacity = face_blocks.shape[0] // NS
    n_elems, rows, lanes = adjoint.shape
    width = face_blocks.shape[2]
    tables = (face_left, face_right, face_code, side_counts)
    sums = jax.ShapeDtypeStruct((n_elems, rows, lanes), jnp.bfloat16)
    totals = jax.ShapeDtypeStruct((n_elems, rows, lanes), jnp.float32)

    def call(kernel, in_specs, out_shape, blocks, scratch=()):
        return pl.pallas_call(
            kernel,
            in_specs=in_specs,
            out_specs=[vmem] * len(out_shape),
            scratch_shapes=[pltpu.VMEM((n_elems + 1, rows, lanes), jnp.float32), *scratch],
            out_shape=out_shape,
            cost_estimate=pl.CostEstimate(
                flops=2 * blocks * rows * width * lanes,
                bytes_accessed=2 * blocks * rows * width,
                transcendentals=0,
            ),
            compiler_params=pltpu.CompilerParams(vmem_limit_bytes=8 << 20),
        )

    vmem, away = pl.BlockSpec(memory_space=pltpu.VMEM), pl.BlockSpec(memory_space=pltpu.HBM)
    lists = [pl.BlockSpec(memory_space=pltpu.SMEM)] * 4
    fetched = [
        pltpu.VMEM((capacity, rows, width), jnp.bfloat16),
        *(pltpu.SMEM(a.shape, a.dtype) for a in tables),
        pltpu.SemaphoreType.DMA((5,)),
    ]
    fetch_pass = call(fetch_pass_kernel, [away] * 4 + [vmem, away], [sums], capacity, fetched)
    pass_on = call(pass_kernel, lists + [vmem] * 2, [sums], capacity)
    rest = call(rest_kernel, lists + [vmem] * 2, [sums] * 2 + [totals], 3 * capacity)
    own = call(own_kernel, lists + [vmem] * 3, [totals], n_elems + capacity)
    ring = [(i, (i + (4 * (i // stride % 2) - 2) * stride) % n_domains) for i in range(n_domains)]
    across = [(i, (i + stride) % (2 * stride) + i // (2 * stride) * 2 * stride) for i in range(n_domains)]
    off_chip = [(i, (i + 2 * (i % 2) - 1) % n_domains) for i in range(n_domains)]
    on_chip = [(i, i + 1 - 2 * (i % 2)) for i in range(n_domains)]
    blocks = pltpu.with_memory_space_constraint(face_blocks, pltpu.VMEM)
    far_off = [pltpu.with_memory_space_constraint(a, pltpu.HBM) for a in (*tables, face_blocks)]
    diag = pltpu.with_memory_space_constraint(diag_blocks, pltpu.VMEM)

    def apply_op(vector, fetch):
        whole = lax.all_gather(vector, "field", axis=1, tiled=True)
        whole = pltpu.with_memory_space_constraint(whole, pltpu.VMEM)
        (passed,) = fetch_pass(*far_off[:4], whole, far_off[4]) if fetch else pass_on(*tables, whole, blocks)
        passed = lax.ppermute(passed, "dom", ring)
        off, on, kept = rest(*tables, whole, blocks)
        off = lax.ppermute(off, "dom", off_chip)
        on = lax.ppermute(on, "dom", on_chip)
        joined = (kept + passed).astype(jnp.bfloat16)
        far = lax.ppermute(joined, "dom", across)
        (total,) = own(*tables, whole, diag, blocks)
        return total + off + on + far

    first = apply_op(adjoint, True)
    psi = (adjoint.astype(jnp.float32) - 0.5 * first).astype(jnp.bfloat16)
    second = apply_op(psi, False).astype(jnp.bfloat16)
    return (psi, second)


def solution(mesh):
    return jax.shard_map(
        local,
        mesh=mesh,
        in_specs=(
            P("dom", "field", None),
            P("dom", "field", None),
            P("dom", "field", None),
            P("dom"),
            P("dom"),
            P("dom"),
            P("dom", None),
        ),
        out_specs=(P("dom", "field", None), P("dom", "field", None)),
        check_vma=False,
    )
```
